32 devices in a mesh: spec: 4 (over z), space: 8 (over y, x, core).
Axes of the slice: x: 2, y: 2, z: 4, core: 2. Of those that a mesh axis runs over, the one named last changes fastest.
Arguments:
- spectrum: bfloat16 [1296, 128, 256], P('spec', 'space'), may hold values from 0.049804688 to 1
- land_sea: int32 [128, 256], P('space'), may hold values from 0 to 1, as said below
- owners: int32 [4], replicated, may hold values from 0 to 3, each once
- proj_weight: bfloat16 [512, 1296], replicated, may hold values from -0.15625 to 0.15625
- back_weight: bfloat16 [1296, 512], replicated, may hold values from -0.25 to 0.25
- ocean_vel: float32 [2, 32, 4, 8, 1024], P(None, None, 'spec', 'space'), may hold values from -4 to 4
- mixing: float32 [32, 4, 8, 1024], P(None, 'spec', 'space'), may hold values from 0.03 to 0.25
- active_layers: int32 [4, 8, 1024], P('spec', 'space'), may hold values from 1 to 32
Outputs:
- new_spectrum: bfloat16 [1296, 128, 256], P('spec', 'space')
- new_ocean: float32 [2, 32, 4, 8, 1024], P(None, None, 'spec', 'space')
The draws below stay inside these ranges and needn't reach their ends.
Inputs may be any that keep to these rules, and one draw needn't show every extreme that they name: `land_sea`: in every aligned block of 4 rows (1024 points) at most 768 points are sea; some block has exactly 768. `owners`: A permutation: the ocean slots of a strip cover its 4 blocks once each.
All inputs are finite; a program needn't handle non-finite values.
Results may differ from the reference program's by a relative error of at most 0.0064.
Values may be sent and summed in bfloat16 or wider, within the bound.
A program may use at most 64 MiB of HBM per device.

```python
import math
import jax
import jax.numpy as jnp
from jax import lax

NDIR = 36
NFREQ = 36
K = 1296
RANK = 512
LAYERS = 32
STEPS = 2
RX = 16
NY = 256
SLOTS = 4
STRIPS = 8
PTS = 1024
CAP = 768
NX = 128
NBLK = 32
PROFILE = 66
N_SPEC = 4
N_SPACE = 8


def draw_land_sea(key, part):
    count_key, full_key, perm_key = jax.random.split(key, 3)
    counts = jax.random.randint(count_key, (NBLK,), PTS // 4, CAP + 1)
    chosen = jax.random.randint(full_key, (), 0, NBLK)
    counts = jnp.where(jnp.arange(NBLK) == chosen, CAP, counts)

    def block_ranks(block_key):
        return jax.random.permutation(block_key, PTS)
    rank_values = jax.vmap(block_ranks)(jax.random.split(perm_key, NBLK))
    sea_points = (rank_values < counts[:, None]).astype(jnp.int32)
    return sea_points.reshape(NX, NY)


def place_ends(result, stream_key, smallest, largest):
    index_at = [jax.random.randint(jax.random.fold_in(stream_key, axis), (), 0, length) for axis, length in enumerate(result.shape)]
    longest = result.shape.index(max(result.shape))
    next_to = index_at[:longest] + [(index_at[longest] + 1) % result.shape[longest]] + index_at[longest + 1:]
    return result.at[tuple(index_at)].set(smallest).at[tuple(next_to)].set(largest)


def steps_of(stream_key, extent, cuts, low, top_value):
    factor_of = 1.0
    for dim, shards_of in cuts:
        steps = jax.random.uniform(jax.random.fold_in(jax.random.fold_in(stream_key, 6), dim), (shards_of,), jnp.float32, low / len(cuts), top_value / len(cuts))
        factor_of = factor_of * jnp.repeat(jnp.exp(steps), extent[dim] // shards_of).reshape((-1,) + (1,) * (len(extent) - 1 - dim))
    return factor_of


def gaussian(own_key, shape, scale, reach, shards=(), held_as=jnp.bfloat16):
    loudness = steps_of(own_key, shape, shards, -0.22, 0.18) if shards else 1.0
    entries = jax.random.normal(own_key, shape, jnp.float32) * scale * loudness
    return jnp.minimum(jnp.maximum(entries, -reach), reach).astype(held_as)


def setup_inputs(seed: int = 0) -> dict:
    seeds = jax.random.split(jax.random.key(seed), 9)
    spectrum = jnp.clip(jnp.exp(math.log(1.0) - 2.9996462 * jax.random.uniform(seeds[0], (K, NX, NY), jnp.float32) ** steps_of(seeds[0], (K, NX, NY), ((0, 4), (1, 8)), -0.2, 0.2)), 0.049804688, 1.0).astype(jnp.bfloat16)
    land_sea = draw_land_sea(jax.random.fold_in(seeds[8], 71), 0)
    owners = jax.random.permutation(seeds[2], SLOTS).astype(jnp.int32)
    proj_weight = gaussian(seeds[3], (RANK, K), K ** -0.5, 0.15625)
    back_weight = gaussian(seeds[4], (K, RANK), RANK ** -0.5, 0.25)
    ocean_vel = gaussian(seeds[5], (2, LAYERS, SLOTS, STRIPS, PTS), 1.0, 4.0, ((2, 4), (3, 8)), jnp.float32)
    mixing = jnp.clip(jnp.exp(math.log(0.25) - 2.1202636 * jax.random.uniform(seeds[6], (LAYERS, SLOTS, STRIPS, PTS), jnp.float32) ** steps_of(seeds[6], (LAYERS, SLOTS, STRIPS, PTS), ((1, 4), (2, 8)), -0.2, 0.2)), 0.03, 0.25)
    active_layers = place_ends(jax.random.randint(seeds[7], (SLOTS, STRIPS, PTS), 1, LAYERS + 1), jax.random.fold_in(seeds[7], 1), 1, LAYERS).astype(jnp.int32)
    return {"spectrum": spectrum, "land_sea": land_sea, "owners": owners, "proj_weight": proj_weight, "back_weight": back_weight, "ocean_vel": ocean_vel, "mixing": mixing, "active_layers": active_layers}


courant_scale = 0.5
current_scale = 0.15
source_step = 0.25
coriolis = 0.3
stress_scale = 0.5
drift_scale = 4.0

def component_tables():
    component = jnp.arange(K, dtype=jnp.int32)
    frequency = component // NDIR
    direction = component % NDIR
    angle = (direction.astype(jnp.float32) + 0.5) * (2.0 * math.pi / NDIR)
    group_speed = courant_scale * jnp.exp(-2.0 * frequency.astype(jnp.float32) / NFREQ)
    eastward = (4 * direction + 2 < NDIR) | (4 * direction + 2 > 3 * NDIR)
    northward = 2 * direction + 1 < NDIR
    return (group_speed * jnp.cos(angle), group_speed * jnp.sin(angle), eastward, northward)

def coupling_tables():
    component = jnp.arange(K, dtype=jnp.int32)
    frequency = (component // NDIR).astype(jnp.float32)
    direction = (component % NDIR).astype(jnp.float32)
    angle = (direction + 0.5) * (2.0 * math.pi / NDIR)
    wavenum = 0.02 * jnp.exp(6.0 * frequency / NFREQ)
    depth = jnp.arange(LAYERS, dtype=jnp.float32)[:, None] + 0.5
    decay_rows = wavenum[None, :] ** 1.5 * jnp.exp(-2.0 * wavenum[None, :] * depth)
    decay_rows = decay_rows / jnp.sqrt(lax.optimization_barrier(jnp.sum(decay_rows * decay_rows, axis=1, keepdims=True)))
    drift_rows = drift_scale * jnp.concatenate([decay_rows * jnp.cos(angle)[None, :], decay_rows * jnp.sin(angle)[None, :]], 0)
    stress = wavenum / jnp.sqrt(jnp.sum(wavenum * wavenum))
    stress_rows = -stress_scale * jnp.stack([stress * jnp.cos(angle), stress * jnp.sin(angle)], 0)
    return (drift_rows, stress_rows)

def face_difference(padded, forward_mask, axis):
    face_count = padded.shape[axis] - 4
    cell_before = lax.slice_in_dim(padded, 0, face_count + 1, axis=axis)
    cell_left = lax.slice_in_dim(padded, 1, face_count + 2, axis=axis)
    cell_right = lax.slice_in_dim(padded, 2, face_count + 3, axis=axis)
    cell_after = lax.slice_in_dim(padded, 3, face_count + 4, axis=axis)
    forward = (5.0 * cell_left + 2.0 * cell_right - cell_before) / 6.0
    backward = (2.0 * cell_left + 5.0 * cell_right - cell_after) / 6.0
    face_flux = jnp.where(forward_mask, forward, backward)
    return lax.slice_in_dim(face_flux, 1, face_count + 1, axis=axis) - lax.slice_in_dim(face_flux, 0, face_count, axis=axis)

def propagate(spectral_state, land_mask, currents, speed_east, speed_north, eastward, northward):
    masked = spectral_state.astype(jnp.float32) * land_mask
    flux_east = (speed_east[:, None, None] + current_scale * currents[0]) * masked
    flux_north = (speed_north[:, None, None] + current_scale * currents[1]) * masked
    padded_east = jnp.pad(flux_east, ((0, 0), (2, 2), (0, 0)))
    padded_north = jnp.pad(flux_north, ((0, 0), (0, 0), (2, 2)))
    advected = masked - face_difference(padded_east, eastward[:, None, None], 1) - face_difference(padded_north, northward[:, None, None], 2)
    return (advected * land_mask).astype(jnp.bfloat16)

def source_block(drift_block, proj_weight, back_weight, drift_rows, stress_rows):
    projected = jnp.dot(proj_weight, drift_block, preferred_element_type=jnp.float32)
    cubed = (projected * projected * projected).astype(jnp.bfloat16)
    transfer = jnp.dot(back_weight, cubed, preferred_element_type=jnp.float32)
    updated = drift_block.astype(jnp.float32) + source_step * transfer
    payload = jnp.concatenate([jnp.dot(drift_rows, updated, precision=lax.Precision.HIGHEST), jnp.dot(stress_rows, transfer, precision=lax.Precision.HIGHEST)], 0)
    return (updated.astype(jnp.bfloat16), payload)

def ocean_step(velocity, payload, mixing, active):
    layer_index = lax.broadcasted_iota(jnp.int32, mixing.shape, 0)
    live_layer = (layer_index < active[None]).astype(jnp.float32)
    bottom = (layer_index == active[None] - 1).astype(jnp.float32)
    surface = (layer_index == 0).astype(jnp.float32)
    upper_mix = mixing[:-1] * live_layer[1:]

    def mixed(field):
        between = upper_mix * (field[:-1] - field[1:])
        inflow = jnp.concatenate([jnp.zeros_like(between[:1]), between], 0)
        outflow = jnp.concatenate([between, jnp.zeros_like(between[:1])], 0)
        return inflow - outflow - mixing * bottom * field
    east_vel = velocity[0]
    north_vel = velocity[1]
    drift_east = payload[:LAYERS]
    drift_north = payload[LAYERS:2 * LAYERS]
    stress_east = payload[2 * LAYERS][None]
    stress_north = payload[2 * LAYERS + 1][None]
    new_east = live_layer * (east_vel + coriolis * (north_vel + drift_north) + mixed(east_vel) + surface * stress_east)
    new_north = live_layer * (north_vel - coriolis * (east_vel + drift_east) + mixed(north_vel) + surface * stress_north)
    return jnp.stack([new_east, new_north], 0)

def reference(spectrum, land_sea, owners, proj_weight, back_weight, ocean_vel, mixing, active_layers):
    speed_east, speed_north, eastward, northward = component_tables()
    drift_rows, stress_rows = coupling_tables()
    land_mask = land_sea.astype(jnp.float32)
    inverse = jnp.argsort(owners).astype(jnp.int32)
    velocity = ocean_vel
    spectral_state = spectrum
    for step_index in range(STEPS):
        surface = jnp.transpose(velocity[:, 0], (0, 2, 1, 3))
        currents = surface[:, :, inverse].reshape(2, NX, NY)
        drifted = propagate(spectral_state, land_mask, currents, speed_east, speed_north, eastward, northward)

        def per_strip(strip_index):
            block = lax.dynamic_slice_in_dim(drifted, strip_index * RX, RX, 1).reshape(K, RX * NY)
            return source_block(block, proj_weight, back_weight, drift_rows, stress_rows)
        new_blocks, payloads = lax.map(per_strip, jnp.arange(N_SPACE, dtype=jnp.int32))
        spectral_state = jnp.transpose(new_blocks, (1, 0, 2)).reshape(K, NX, NY)
        payloads = payloads.reshape(N_SPACE, PROFILE, N_SPEC, PTS)[:, :, owners]
        payloads = jnp.transpose(payloads, (1, 2, 0, 3))
        velocity = ocean_step(velocity, payloads, mixing, active_layers)
    return (spectral_state, velocity)
```

```python
import functools
import math

import jax
import jax.numpy as jnp
from jax import lax
from jax.experimental import pallas as pl
from jax.experimental.pallas import tpu as pltpu
from jax.sharding import PartitionSpec as P

NDIR = 36
NFREQ = 36
K = NDIR * NFREQ
STEPS = 2

courant_scale = 0.5
current_scale = 0.15
source_step = 0.25
coriolis = 0.3
stress_scale = 0.5
drift_scale = 4.0

MESH = pl.DeviceIdType.MESH
F32 = jnp.float32
BF16 = jnp.bfloat16
VMEM_LIMIT = 60 * 1024 * 1024
ROWS = 16


def tap_tables(first, count, padded):
    component = jnp.minimum(first + jnp.arange(padded, dtype=jnp.int32), K - 1)
    frequency = component // NDIR
    direction = component % NDIR
    angle = (direction.astype(F32) + 0.5) * (2.0 * math.pi / NDIR)
    speed = courant_scale * jnp.exp(-2.0 * frequency.astype(F32) / NFREQ)
    eastward = (4 * direction + 2 < NDIR) | (4 * direction + 2 > 3 * NDIR)
    northward = 2 * direction + 1 < NDIR
    forward = (1.0 / 6.0, -1.0, 0.5, 2.0 / 6.0, 0.0)
    backward = (0.0, -2.0 / 6.0, -0.5, 1.0, -1.0 / 6.0)
    columns = [speed * jnp.cos(angle), speed * jnp.sin(angle)]
    for mask in (eastward, northward):
        for f, b in zip(forward, backward):
            columns.append(jnp.where(mask, F32(f), F32(b)))
    return jnp.stack(columns, 1)


def coupling_tables(layers):
    component = jnp.arange(K, dtype=jnp.int32)
    frequency = (component // NDIR).astype(F32)
    direction = (component % NDIR).astype(F32)
    angle = (direction + 0.5) * (2.0 * math.pi / NDIR)
    wavenum = 0.02 * jnp.exp(6.0 * frequency / NFREQ)
    depth = jnp.arange(layers, dtype=F32)[:, None] + 0.5
    decay_rows = wavenum[None, :] ** 1.5 * jnp.exp(-2.0 * wavenum[None, :] * depth)
    decay_rows = decay_rows / jnp.sqrt(jnp.sum(decay_rows * decay_rows, axis=1, keepdims=True))
    drift_rows = drift_scale * jnp.concatenate(
        [decay_rows * jnp.cos(angle)[None, :], decay_rows * jnp.sin(angle)[None, :]], 0
    )
    stress = wavenum / jnp.sqrt(jnp.sum(wavenum * wavenum))
    stress_rows = -stress_scale * jnp.stack([stress * jnp.cos(angle), stress * jnp.sin(angle)], 0)
    return (drift_rows, stress_rows)


def pieces(rows):
    first = lax.reduce_precision(rows, 8, 7)
    rest = rows - first
    second = lax.reduce_precision(rest, 8, 7)
    third = rest - second
    return jnp.concatenate([first, second, third], 0).astype(BF16)


def advect_kernel(width, owners, state, before, after, land, east, north, taps, rank, out, drift):
    slots, chunks, comps, chunk_width = out.shape
    padded, points = state.shape
    rows = points // width
    block = points // slots
    column = lax.broadcasted_iota(jnp.int32, (ROWS, width), 1)

    def shifted(value, by):
        turned = pltpu.roll(value, by % width, 1)
        inside = (column >= by) if by > 0 else (column < width + by)
        return jnp.where(inside, turned, 0.0)

    def chunk(index, carry):
        here = pl.ds(pl.multiple_of(index * ROWS, ROWS), ROWS)
        tap = taps[here, :]

        def spread(i):
            return jnp.broadcast_to(tap[:, i : i + 1], (ROWS, width))

        speed_east, speed_north = spread(0), spread(1)
        row_tap = [spread(2 + i) for i in range(5)]
        col_tap = [spread(7 + i) for i in range(5)]

        def masked_row(r):
            if r < 0:
                return before[here, (r + 2) * width : (r + 3) * width].astype(F32)
            if r >= rows:
                return after[here, (r - rows) * width : (r - rows + 1) * width].astype(F32)
            at = slice(r * width, (r + 1) * width)
            return state[here, at].astype(F32) * land[:, at]

        def flux(r, masked):
            at = slice((r + 2) * width, (r + 3) * width)
            return (speed_east + current_scale * east[:, at]) * masked

        masked = {}
        flow = {}
        for r in range(-2, rows + 2):
            masked[r] = masked_row(r)
            flow[r] = flux(r, masked[r])
            c = r - 2
            if c < 0:
                continue
            at = slice(c * width, (c + 1) * width)
            m = masked.pop(c)
            along = (speed_north + current_scale * north[:, at]) * m
            total = m
            for i in range(5):
                total = total - row_tap[i] * flow[c - 2 + i]
            total = total - col_tap[2] * along
            for i in (0, 1, 3, 4):
                total = total - col_tap[i] * shifted(along, 2 - i)
            flow.pop(c - 2)
            b, inner = c * width // block, c * width % block
            drift[b, here, inner : inner + width] = (total * land[:, at]).astype(BF16)
        return carry

    lax.fori_loop(0, padded // ROWS, chunk, 0)

    position = lax.broadcasted_iota(jnp.int32, (chunks * chunk_width, block), 0)

    def pack(s, carry):
        b = owners[s]
        spot = (position == rank[b]).astype(F32).astype(BF16)
        packed = lax.dot_general(
            drift[b], spot, (((1,), (1,)), ((), ())), preferred_element_type=F32
        ).astype(BF16)
        for j in range(chunks):
            out[s, j] = packed[:comps, j * chunk_width : (j + 1) * chunk_width]
        return carry

    lax.fori_loop(0, slots, pack, 0)


def expand_kernel(inverse, packed, rank, out):
    chunks, slots, comps, chunk_width = packed.shape
    padded, block = out.shape[1:]
    position = lax.broadcasted_iota(jnp.int32, (chunk_width, block), 0)

    def expand(b, carry):
        s = inverse[b]
        total = jnp.zeros((comps, block), F32)
        for j in range(chunks):
            spot = (position + j * chunk_width == rank[b]).astype(F32).astype(BF16)
            total = total + jnp.dot(packed[j, s], spot, preferred_element_type=F32)
        out[b, :comps, :] = total.astype(BF16)
        if padded > comps:
            out[b, comps:, :] = jnp.zeros((padded - comps, block), BF16)
        return carry

    lax.fori_loop(0, slots, expand, 0)


def source_kernel(
    layers, blocks, proj, back, inner, velocity, mixing, active, rank,
    returned, new_velocity, surfaces,
    got, made, pay, surface,
    send_in, recv_in, send_back, recv_back, send_top, recv_top,
):
    slots, chunks, comps, chunk_width = blocks.shape
    rank_rows = back.shape[2]
    points = rank.shape[1]
    me = lax.axis_index("spec")

    def peer(delta):
        return lax.rem(me + delta, slots)

    barrier = pltpu.get_barrier_semaphore()
    for delta in range(1, slots):
        pl.semaphore_signal(
            barrier, inc=1, device_id={"spec": peer(delta)}, device_id_type=MESH
        )
    pl.semaphore_wait(barrier, slots - 1)

    def inward(j, delta):
        return pltpu.make_async_remote_copy(
            src_ref=blocks.at[peer(delta), j],
            dst_ref=got.at[j, me],
            send_sem=send_in.at[j, delta],
            recv_sem=recv_in.at[j, delta],
            device_id={"spec": peer(delta)},
            device_id_type=MESH,
        )

    def homeward(j, delta):
        return pltpu.make_async_remote_copy(
            src_ref=made.at[j, peer(delta)],
            dst_ref=returned.at[j, me],
            send_sem=send_back.at[j, delta],
            recv_sem=recv_back.at[j, delta],
            device_id={"spec": peer(delta)},
            device_id_type=MESH,
        )

    for j in range(chunks):
        for delta in range(1, slots):
            inward(j, delta).start()
    for j in range(chunks):
        got[j, me] = blocks[me, j]

    def one_chunk(j, carry):
        for delta in range(1, slots):
            inward(j, delta).wait_recv()
        full = jnp.dot(proj[0], got[j, 0], preferred_element_type=F32)
        for g in range(1, slots):
            full = full + jnp.dot(proj[g], got[j, g], preferred_element_type=F32)
        projected = full[:rank_rows]
        cubed = (projected * projected * projected).astype(BF16)
        for delta in list(range(1, slots)) + [0]:
            g = peer(delta)
            transfer = jnp.dot(back[g], cubed, preferred_element_type=F32)
            updated = (got[j, g].astype(F32) + source_step * transfer).astype(BF16)
            made[j, g] = updated
            if delta:
                homeward(j, delta).start()
            else:
                returned[j, g] = updated
        drift = full[rank_rows:]
        third = drift.shape[0] // 3
        drift = drift[:third] + drift[third : 2 * third] + drift[2 * third :]
        more = jnp.dot(inner[...], cubed, preferred_element_type=F32)
        third = more.shape[0] // 3
        pay[j] = drift + (more[:third] + more[third : 2 * third] + more[2 * third :])
        return carry

    lax.fori_loop(0, chunks, one_chunk, 0)

    position = lax.broadcasted_iota(jnp.int32, (chunk_width, points), 0)
    payload = None
    for j in range(chunks):
        spot = (position + j * chunk_width == rank[...]).astype(F32).astype(BF16)
        value = pay[j]
        for _ in range(3):
            part = value.astype(BF16)
            value = value - part.astype(F32)
            term = jnp.dot(part, spot, preferred_element_type=F32)
            payload = term if payload is None else payload + term

    layer = lax.broadcasted_iota(jnp.int32, (layers, points), 0)
    depth = active[...]
    live = (layer < depth).astype(F32)
    bottom = (layer == depth - 1).astype(F32)
    top = (layer == 0).astype(F32)
    mix = mixing[...]
    upper = mix * ((layer + 1 < depth) & (layer < layers - 1)).astype(F32)

    def mixed(field):
        between = upper * (field - pltpu.roll(field, layers - 1, 0))
        return pltpu.roll(between, 1, 0) - between - mix * bottom * field

    east, north = velocity[0], velocity[1]
    drift_east = payload[:layers]
    drift_north = payload[layers : 2 * layers]
    stress_east = payload[2 * layers : 2 * layers + 1]
    stress_north = payload[2 * layers + 1 : 2 * layers + 2]
    new_east = live * (east + coriolis * (north + drift_north) + mixed(east) + top * stress_east)
    new_north = live * (north - coriolis * (east + drift_east) + mixed(north) + top * stress_north)
    new_velocity[0] = new_east
    new_velocity[1] = new_north
    surface[0:1, :] = new_east[0:1]
    surface[1:2, :] = new_north[0:1]
    surfaces[me] = surface[...]

    def upward(delta):
        return pltpu.make_async_remote_copy(
            src_ref=surface,
            dst_ref=surfaces.at[me],
            send_sem=send_top.at[delta],
            recv_sem=recv_top.at[delta],
            device_id={"spec": peer(delta)},
            device_id_type=MESH,
        )

    for delta in range(1, slots):
        upward(delta).start()
    for delta in range(1, slots):
        upward(delta).wait()
    for j in range(chunks):
        for delta in range(1, slots):
            inward(j, delta).wait_send()
            homeward(j, delta).wait()


def whole(count, memory=pltpu.VMEM):
    return [pl.BlockSpec(memory_space=memory)] * count


def shift_rows(head, tail):
    count = lax.axis_size("space")
    up = [(i, i + 1) for i in range(count - 1)]
    down = [(i + 1, i) for i in range(count - 1)]
    return lax.ppermute(tail, "space", up), lax.ppermute(head, "space", down)


def body(spectrum, land_sea, owners, proj_weight, back_weight, ocean_vel, mixing, active_layers):
    comps, rows, width = spectrum.shape
    slots = lax.axis_size("spec")
    points = rows * width
    block = points // slots
    cap = block * 3 // 4
    chunk_width = 256 if cap % 256 == 0 else cap
    chunks = cap // chunk_width
    layers = mixing.shape[0]
    rank_rows = proj_weight.shape[0]
    padded = -(-comps // ROWS) * ROWS
    me = lax.axis_index("spec")

    inverse = jnp.sum(
        jnp.where(owners[:, None] == jnp.arange(slots)[None], jnp.arange(slots)[:, None], 0), 0
    ).astype(jnp.int32)
    taps = tap_tables(me * comps, comps, padded)
    drift_rows, stress_rows = coupling_tables(layers)
    zeros = jnp.zeros((6, K), F32)
    outer_rows = pieces(jnp.concatenate([drift_rows, zeros, zeros[:2]], 0))
    through = jnp.dot(
        jnp.concatenate([source_step * drift_rows, stress_rows, zeros], 0),
        back_weight.astype(F32),
        precision=lax.Precision.HIGHEST,
    )
    inner = pieces(through)
    proj = jnp.concatenate([proj_weight, outer_rows], 0)
    proj = jnp.transpose(proj.reshape(proj.shape[0], slots, comps), (1, 0, 2))
    back = back_weight.reshape(slots, comps, rank_rows)

    land = land_sea.astype(F32).reshape(1, points)
    sea = land_sea.reshape(slots, block)
    rank = jnp.where(sea > 0, jnp.cumsum(sea, 1) - 1, -1).reshape(slots, 1, block)
    my_rank = lax.dynamic_index_in_dim(rank, owners[me], 0, False)

    velocity = ocean_vel.reshape(2, layers, block)
    mixing_local = mixing.reshape(layers, block)
    active = active_layers.reshape(1, block)
    surfaces = lax.all_gather(velocity[:, 0], "spec", axis=0)
    head = (spectrum[:, :2] * land_sea[None, :2].astype(BF16)).reshape(comps, 2 * width)
    tail = (spectrum[:, -2:] * land_sea[None, -2:].astype(BF16)).reshape(comps, 2 * width)
    state = jnp.pad(spectrum.reshape(comps, points), ((0, padded - comps), (0, 0)))
    for _ in range(STEPS):
        before, after = shift_rows(head, tail)
        before = jnp.pad(before, ((0, padded - comps), (0, 0)))
        after = jnp.pad(after, ((0, padded - comps), (0, 0)))
        currents = sum(
            jnp.where((owners[s] == jnp.arange(slots))[:, None, None], surfaces[s][None], 0.0)
            for s in range(slots)
        )
        east = currents[:, 0].reshape(1, points)
        north = currents[:, 1].reshape(1, points)
        east_before, east_after = shift_rows(east[:, : 2 * width], east[:, -2 * width :])
        east = jnp.concatenate([east_before, east, east_after], 1)
        blocks = pl.pallas_call(
            functools.partial(advect_kernel, width),
            out_shape=jax.ShapeDtypeStruct((slots, chunks, comps, chunk_width), BF16),
            in_specs=whole(1, pltpu.SMEM) + whole(8),
            out_specs=pl.BlockSpec(memory_space=pltpu.VMEM),
            scratch_shapes=[pltpu.VMEM((slots, padded, block), BF16)],
            compiler_params=pltpu.CompilerParams(vmem_limit_bytes=VMEM_LIMIT),
            name="advect",
        )(owners, state, before, after, land, east, north, taps, rank)
        returned, velocity, surfaces = pl.pallas_call(
            functools.partial(source_kernel, layers),
            out_shape=(
                jax.ShapeDtypeStruct((chunks, slots, comps, chunk_width), BF16),
                jax.ShapeDtypeStruct((2, layers, block), F32),
                jax.ShapeDtypeStruct((slots, 2, block), F32),
            ),
            in_specs=whole(8),
            out_specs=tuple(whole(3)),
            scratch_shapes=[
                pltpu.VMEM((chunks, slots, comps, chunk_width), BF16),
                pltpu.VMEM((chunks, slots, comps, chunk_width), BF16),
                pltpu.VMEM((chunks, inner.shape[0] // 3, chunk_width), F32),
                pltpu.VMEM((2, block), F32),
                pltpu.SemaphoreType.DMA((chunks, slots)),
                pltpu.SemaphoreType.DMA((chunks, slots)),
                pltpu.SemaphoreType.DMA((chunks, slots)),
                pltpu.SemaphoreType.DMA((chunks, slots)),
                pltpu.SemaphoreType.DMA((slots,)),
                pltpu.SemaphoreType.DMA((slots,)),
            ],
            compiler_params=pltpu.CompilerParams(
                vmem_limit_bytes=VMEM_LIMIT, collective_id=0, has_side_effects=True
            ),
            name="source",
        )(blocks, proj, back, inner, velocity, mixing_local, active, my_rank)
        grid = pl.pallas_call(
            expand_kernel,
            out_shape=jax.ShapeDtypeStruct((slots, padded, block), BF16),
            in_specs=whole(1, pltpu.SMEM) + whole(2),
            out_specs=pl.BlockSpec(memory_space=pltpu.VMEM),
            compiler_params=pltpu.CompilerParams(vmem_limit_bytes=VMEM_LIMIT),
            name="expand",
        )(inverse, returned, rank)
        state = jnp.transpose(grid, (1, 0, 2)).reshape(padded, points)
        head = state[:comps, : 2 * width]
        tail = state[:comps, -2 * width :]
    return (state[:comps].reshape(comps, rows, width), velocity.reshape(ocean_vel.shape))


def solution(mesh):
    placed = (
        P("spec", "space", None),
        P("space", None),
        P(),
        P(),
        P(),
        P(None, None, "spec", "space", None),
        P(None, "spec", "space", None),
        P("spec", "space", None),
    )
    return jax.shard_map(
        body,
        mesh=mesh,
        in_specs=placed,
        out_specs=(P("spec", "space", None), P(None, None, "spec", "space", None)),
        check_vma=False,
    )
```

```python
import functools
import math

import jax
import jax.numpy as jnp
import numpy as np
from jax import lax
from jax.experimental import pallas as pl
from jax.experimental.pallas import tpu as pltpu
from jax.sharding import PartitionSpec as P

NDIR = 36
NFREQ = 36
K = NDIR * NFREQ
STEPS = 2

courant_scale = 0.5
current_scale = 0.15
source_step = 0.25
coriolis = 0.3
stress_scale = 0.5
drift_scale = 4.0

MESH = pl.DeviceIdType.MESH
F32 = jnp.float32
BF16 = jnp.bfloat16
VMEM_LIMIT = 60 * 1024 * 1024
ROWS = 16


def tap_table():
    component = np.arange(K)
    frequency = component // NDIR
    direction = component % NDIR
    angle = (direction + 0.5) * (2.0 * math.pi / NDIR)
    speed = courant_scale * np.exp(-2.0 * frequency / NFREQ)
    eastward = (4 * direction + 2 < NDIR) | (4 * direction + 2 > 3 * NDIR)
    northward = 2 * direction + 1 < NDIR
    forward = (1.0 / 6.0, -1.0, 0.5, 2.0 / 6.0, 0.0)
    backward = (0.0, -2.0 / 6.0, -0.5, 1.0, -1.0 / 6.0)
    columns = [speed * np.cos(angle), speed * np.sin(angle)]
    for mask in (eastward, northward):
        for f, b in zip(forward, backward):
            columns.append(np.where(mask, f, b))
    return np.stack(columns, 1).astype(np.float32)


def coupling_tables(layers):
    component = np.arange(K)
    frequency = component // NDIR
    angle = (component % NDIR + 0.5) * (2.0 * math.pi / NDIR)
    wavenum = 0.02 * np.exp(6.0 * frequency / NFREQ)
    depth = np.arange(layers)[:, None] + 0.5
    decay_rows = wavenum[None, :] ** 1.5 * np.exp(-2.0 * wavenum[None, :] * depth)
    decay_rows = decay_rows / np.sqrt(np.sum(decay_rows * decay_rows, axis=1, keepdims=True))
    drift_rows = drift_scale * np.concatenate(
        [decay_rows * np.cos(angle)[None, :], decay_rows * np.sin(angle)[None, :]], 0
    )
    stress = wavenum / np.sqrt(np.sum(wavenum * wavenum))
    stress_rows = -stress_scale * np.stack([stress * np.cos(angle), stress * np.sin(angle)], 0)
    return (drift_rows.astype(np.float32), stress_rows.astype(np.float32))


def pieces(rows):
    first = lax.reduce_precision(rows, 8, 7)
    rest = rows - first
    second = lax.reduce_precision(rest, 8, 7)
    third = rest - second
    return jnp.concatenate([first, second, third], 0).astype(BF16)


def constant_pieces(rows):
    first = rows.astype(BF16)
    rest = rows - first.astype(np.float32)
    second = rest.astype(BF16)
    third = (rest - second.astype(np.float32)).astype(BF16)
    return np.concatenate([first, second, third], 0)


def step_kernel(
    width, owners, inverse, state, land, place, rank, my_rank, taps, proj, outer, back, inner, velocity, mixing, active,
    out, new_velocity,
    field, east, north, drift, blocks, got, made, returned, pay, surface, surfaces,
    head, tail, before, after, east_head, east_tail, east_before, east_after,
    send_in, recv_in, send_back, recv_back, send_top, recv_top, send_edge, recv_edge,
):
    slots, chunks, comps, chunk_width = blocks.shape
    padded = field.shape[1]
    points = state.shape[1]
    block = points // slots
    block_rows = block // width
    rank_rows = back.shape[2]
    layers = mixing.shape[0]
    me = lax.axis_index("spec")
    strip = lax.axis_index("space")
    strips = lax.axis_size("space")
    edge = 2 * width
    has_before = strip > 0
    has_after = strip < strips - 1

    def peer(delta):
        return lax.rem(me + delta, slots)

    def spread_out(target, rows_at, low, value):
        for b in range(slots):
            start, stop = b * block, (b + 1) * block + 2 * edge
            first, last = max(start, low), min(stop, low + value.shape[1])
            if first < last:
                target[b, rows_at, first - start : last - start] = value[:, first - low : last - low]

    def copy(source, target, send, receive, device):
        return pltpu.make_async_remote_copy(
            src_ref=source, dst_ref=target, send_sem=send, recv_sem=receive,
            device_id=device, device_id_type=MESH,
        )

    def inward(j, delta):
        return copy(
            blocks.at[peer(delta), j], got.at[j, me],
            send_in.at[j, delta], recv_in.at[j, delta], {"spec": peer(delta)},
        )

    def homeward(j, delta):
        return copy(
            made.at[j, peer(delta)], returned.at[j, me],
            send_back.at[j, delta], recv_back.at[j, delta], {"spec": peer(delta)},
        )

    def upward(delta):
        return copy(
            surface, surfaces.at[me], send_top.at[delta], recv_top.at[delta], {"spec": peer(delta)}
        )

    def to_before(source, target, i):
        return copy(source, target, send_edge.at[i], recv_edge.at[i], {"space": strip - 1})

    def to_after(source, target, i):
        return copy(source, target, send_edge.at[i], recv_edge.at[i], {"space": strip + 1})

    barrier = pltpu.get_barrier_semaphore()
    for delta in range(1, slots):
        pl.semaphore_signal(
            barrier, inc=1, device_id={"spec": peer(delta)}, device_id_type=MESH
        )

    @pl.when(has_before)
    def _():
        pl.semaphore_signal(barrier, inc=1, device_id={"space": strip - 1}, device_id_type=MESH)

    @pl.when(has_after)
    def _():
        pl.semaphore_signal(barrier, inc=1, device_id={"space": strip + 1}, device_id_type=MESH)

    surface[0:1, :] = velocity[0, 0:1, :]
    surface[1:2, :] = velocity[1, 0:1, :]
    everywhere = jnp.concatenate([land[b] for b in range(slots)], 1)
    head[...] = (state[:, :edge].astype(F32) * everywhere[:, :edge]).astype(BF16)
    tail[...] = (state[:, points - edge :].astype(F32) * everywhere[:, points - edge :]).astype(BF16)
    expected = slots - 1 + has_before.astype(jnp.int32) + has_after.astype(jnp.int32)
    pl.semaphore_wait(barrier, expected)

    for delta in range(1, slots):
        upward(delta).start()

    @pl.when(has_before)
    def _():
        to_before(head, after, 0).start()

    @pl.when(has_after)
    def _():
        to_after(tail, before, 1).start()

    surfaces[me] = surface[...]
    whole_chunks = comps // ROWS
    rest = comps - whole_chunks * ROWS

    def fill(index, carry):
        here = pl.ds(pl.multiple_of(index * ROWS, ROWS), ROWS)
        masked = (state[here, :].astype(F32) * everywhere).astype(BF16)
        spread_out(field, here, edge, masked)
        return carry

    lax.fori_loop(0, whole_chunks, fill, 0)
    if rest:
        at = whole_chunks * ROWS
        for b in range(slots):
            field[b, at:, :] = jnp.zeros((padded - at, field.shape[2]), BF16)
        masked = (state[at:, :].astype(F32) * everywhere).astype(BF16)
        spread_out(field, slice(at, comps), edge, masked)

    for delta in range(1, slots):
        upward(delta).wait()
    currents = []
    for b in range(slots):
        here = jnp.zeros((2, block), F32)
        for s in range(slots):
            here = here + place[b, s] * surfaces[s]
        currents.append(here)
        north[b] = here[1:2]
    eastward = jnp.concatenate([here[0:1] for here in currents], 1)
    spread_out(east, slice(0, 1), edge, eastward)
    east_head[...] = eastward[:, :edge]
    east_tail[...] = eastward[:, points - edge :]

    @pl.when(has_before)
    def _():
        to_before(east_head, east_after, 2).start()

    @pl.when(has_after)
    def _():
        to_after(east_tail, east_before, 3).start()

    @pl.when(has_after)
    def _():
        to_after(head, after, 0).wait_recv()
        to_after(east_head, east_after, 2).wait_recv()
        spread_out(field, slice(0, comps), edge + points, after[...])
        spread_out(east, slice(0, 1), edge + points, east_after[...])

    @pl.when(jnp.logical_not(has_after))
    def _():
        spread_out(field, slice(0, comps), edge + points, jnp.zeros((comps, edge), BF16))
        spread_out(east, slice(0, 1), edge + points, jnp.zeros((1, edge), F32))

    @pl.when(has_before)
    def _():
        to_before(tail, before, 1).wait_recv()
        to_before(east_tail, east_before, 3).wait_recv()
        spread_out(field, slice(0, comps), 0, before[...])
        spread_out(east, slice(0, 1), 0, east_before[...])

    @pl.when(jnp.logical_not(has_before))
    def _():
        spread_out(field, slice(0, comps), 0, jnp.zeros((comps, edge), BF16))
        spread_out(east, slice(0, 1), 0, jnp.zeros((1, edge), F32))

    column = lax.broadcasted_iota(jnp.int32, (ROWS, width), 1)
    position = lax.broadcasted_iota(jnp.int32, (chunks * chunk_width, block), 0)

    def shifted(value, by):
        turned = pltpu.roll(value, by % width, 1)
        inside = (column >= by) if by > 0 else (column < width + by)
        return jnp.where(inside, turned, 0.0)

    def advect(b):
        def lanes(r):
            return slice(r * width, (r + 1) * width)

        def chunk(index, carry):
            here = pl.ds(pl.multiple_of(index * ROWS, ROWS), ROWS)
            tap = taps[here, :]

            def spread(i):
                return jnp.broadcast_to(tap[:, i : i + 1], (ROWS, width))

            speed_east, speed_north = spread(0), spread(1)
            row_tap = [spread(2 + i) for i in range(5)]
            col_tap = [spread(7 + i) for i in range(5)]
            masked = {}
            flow = {}
            for r in range(-2, block_rows + 2):
                masked[r] = field[b, here, lanes(r + 2)].astype(F32)
                flow[r] = (speed_east + current_scale * east[b, :, lanes(r + 2)]) * masked[r]
                c = r - 2
                if c < 0:
                    continue
                m = masked.pop(c)
                along = (speed_north + current_scale * north[b, :, lanes(c)]) * m
                total = m
                for i in range(5):
                    total = total - row_tap[i] * flow[c - 2 + i]
                total = total - col_tap[2] * along
                for i in (0, 1, 3, 4):
                    total = total - col_tap[i] * shifted(along, 2 - i)
                flow.pop(c - 2)
                drift[here, c * width : (c + 1) * width] = (total * land[b, :, lanes(c)]).astype(BF16)
            return carry

        lax.fori_loop(0, padded // ROWS, chunk, 0)
        spot = (position == rank[b]).astype(F32).astype(BF16)
        return lax.dot_general(
            drift[...], spot, (((1,), (1,)), ((), ())), preferred_element_type=F32
        ).astype(BF16)

    def one_slot(delta, carry):
        slot = peer(delta)
        packed = advect(owners[slot])

        for j in range(chunks):
            part = packed[:comps, j * chunk_width : (j + 1) * chunk_width]
            blocks[slot, j] = part

        @pl.when(delta < slots)
        def _():
            for j in range(chunks):
                inward(j, delta).start()

        return carry

    lax.fori_loop(1, slots + 1, one_slot, 0)
    for j in range(chunks):
        got[j, me] = blocks[me, j]

    def one_chunk(j, carry):
        for delta in range(1, slots):
            inward(j, delta).wait_recv()
        projected = jnp.dot(proj[0], got[j, 0], preferred_element_type=F32)
        for g in range(1, slots):
            projected = projected + jnp.dot(proj[g], got[j, g], preferred_element_type=F32)
        cubed = (projected * projected * projected).astype(BF16)
        for delta in list(range(1, slots)) + [0]:
            g = peer(delta)
            transfer = jnp.dot(back[g], cubed, preferred_element_type=F32)
            updated = (got[j, g].astype(F32) + source_step * transfer).astype(BF16)
            if delta:
                made[j, g] = updated
                homeward(j, delta).start()
            else:
                returned[j, g] = updated
        more = jnp.dot(inner[...], cubed, preferred_element_type=F32)
        for g in range(slots):
            more = more + jnp.dot(outer[g], got[j, g], preferred_element_type=F32)
        third = more.shape[0] // 3
        pay[j] = more[:third] + more[third : 2 * third] + more[2 * third :]
        return carry

    lax.fori_loop(0, chunks, one_chunk, 0)

    payload = None
    for j in range(chunks):
        spot = lax.broadcasted_iota(jnp.int32, (chunk_width, block), 0) + j * chunk_width
        spot = (spot == my_rank[...]).astype(F32).astype(BF16)
        value = pay[j]
        for _ in range(3):
            part = value.astype(BF16)
            value = value - part.astype(F32)
            term = jnp.dot(part, spot, preferred_element_type=F32)
            payload = term if payload is None else payload + term

    layer = lax.broadcasted_iota(jnp.int32, (layers, block), 0)
    depth = active[...]
    live = (layer < depth).astype(F32)
    bottom = (layer == depth - 1).astype(F32)
    top = (layer == 0).astype(F32)
    mix = mixing[...]
    upper = mix * ((layer + 1 < depth) & (layer < layers - 1)).astype(F32)

    def mixed(value):
        between = upper * (value - pltpu.roll(value, layers - 1, 0))
        return pltpu.roll(between, 1, 0) - between - mix * bottom * value

    old_east, old_north = velocity[0], velocity[1]
    drift_east = payload[:layers]
    drift_north = payload[layers : 2 * layers]
    stress_east = payload[2 * layers : 2 * layers + 1]
    stress_north = payload[2 * layers + 1 : 2 * layers + 2]
    new_velocity[0] = live * (
        old_east + coriolis * (old_north + drift_north) + mixed(old_east) + top * stress_east
    )
    new_velocity[1] = live * (
        old_north - coriolis * (old_east + drift_east) + mixed(old_north) + top * stress_north
    )

    for j in range(chunks):
        for delta in range(1, slots):
            homeward(j, delta).wait_recv()

    for b in range(slots):
        for j in range(chunks):
            spot = lax.broadcasted_iota(jnp.int32, (chunk_width, block), 0) + j * chunk_width
            spot = (spot == rank[b]).astype(F32).astype(BF16)
            term = jnp.dot(returned[j, inverse[b]], spot, preferred_element_type=F32)
            total = term if j == 0 else total + term
        out[:, b * block : (b + 1) * block] = total.astype(BF16)

    @pl.when(has_before)
    def _():
        to_before(head, after, 0).wait_send()
        to_before(east_head, east_after, 2).wait_send()

    @pl.when(has_after)
    def _():
        to_after(tail, before, 1).wait_send()
        to_after(east_tail, east_before, 3).wait_send()

    for j in range(chunks):
        for delta in range(1, slots):
            inward(j, delta).wait_send()
            homeward(j, delta).wait_send()


def whole(count, memory=pltpu.VMEM):
    return [pl.BlockSpec(memory_space=memory)] * count


def body(spectrum, land_sea, owners, proj_weight, back_weight, ocean_vel, mixing, active_layers):
    comps, rows, width = spectrum.shape
    slots = lax.axis_size("spec")
    points = rows * width
    block = points // slots
    cap = block * 3 // 4
    chunk_width = 256 if cap % 256 == 0 else cap
    chunks = cap // chunk_width
    layers = mixing.shape[0]
    rank_rows = proj_weight.shape[0]
    padded = -(-comps // ROWS) * ROWS
    edge = 2 * width
    me = lax.axis_index("spec")

    table = np.zeros((slots, padded, 12), np.float32)
    table[:, :comps] = tap_table().reshape(slots, comps, 12)
    taps = lax.dynamic_index_in_dim(jnp.asarray(table), me, 0, False)
    drift_rows, stress_rows = coupling_tables(layers)
    zeros = np.zeros((6, K), np.float32)
    outer = constant_pieces(np.concatenate([drift_rows, zeros, zeros[:2]], 0))
    outer = jnp.asarray(
        np.ascontiguousarray(outer.reshape(outer.shape[0], slots, comps).transpose(1, 0, 2))
    )
    through = jnp.dot(
        jnp.asarray(np.concatenate([source_step * drift_rows, stress_rows, zeros], 0)),
        back_weight.astype(F32),
        precision=lax.Precision.HIGHEST,
    )
    inner = pieces(through)
    proj = jnp.transpose(proj_weight.reshape(rank_rows, slots, comps), (1, 0, 2))
    back = back_weight.reshape(slots, comps, rank_rows)

    land = land_sea.astype(F32).reshape(slots, 1, block)
    covers = (owners[None, :] == jnp.arange(slots, dtype=jnp.int32)[:, None]).astype(jnp.int32)
    inverse = jnp.sum(covers * jnp.arange(slots, dtype=jnp.int32)[None], 1)
    place = jnp.broadcast_to(covers.astype(F32)[:, :, None, None], (slots, slots, 1, block))
    sea = land_sea.reshape(slots, block)
    rank = jnp.where(sea > 0, jnp.cumsum(sea, 1) - 1, -1).reshape(slots, 1, block)
    my_rank = lax.dynamic_index_in_dim(rank, owners[me], 0, False)

    velocity = ocean_vel.reshape(2, layers, block)
    mixing_local = mixing.reshape(layers, block)
    active = active_layers.reshape(1, block)
    state = spectrum.reshape(comps, points)
    pay_rows = inner.shape[0] // 3
    exchange = pltpu.VMEM((chunks, slots, comps, chunk_width), BF16)
    for _ in range(STEPS):
        state, velocity = pl.pallas_call(
            functools.partial(step_kernel, width),
            out_shape=(
                jax.ShapeDtypeStruct((comps, points), BF16),
                jax.ShapeDtypeStruct((2, layers, block), F32),
            ),
            in_specs=whole(2, pltpu.SMEM) + whole(13),
            out_specs=tuple(whole(2)),
            scratch_shapes=[
                pltpu.VMEM((slots, padded, block + 2 * edge), BF16),
                pltpu.VMEM((slots, 1, block + 2 * edge), F32),
                pltpu.VMEM((slots, 1, block), F32),
                pltpu.VMEM((padded, block), BF16),
                pltpu.VMEM((slots, chunks, comps, chunk_width), BF16),
                exchange,
                exchange,
                exchange,
                pltpu.VMEM((chunks, pay_rows, chunk_width), F32),
                pltpu.VMEM((2, block), F32),
                pltpu.VMEM((slots, 2, block), F32),
            ]
            + [pltpu.VMEM((comps, edge), BF16)] * 4
            + [pltpu.VMEM((1, edge), F32)] * 4
            + [pltpu.SemaphoreType.DMA((chunks, slots))] * 4
            + [pltpu.SemaphoreType.DMA((slots,))] * 2
            + [pltpu.SemaphoreType.DMA((4,))] * 2,
            compiler_params=pltpu.CompilerParams(
                vmem_limit_bytes=VMEM_LIMIT, collective_id=0, has_side_effects=True
            ),
            name="step",
        )(owners, inverse, state, land, place, rank, my_rank, taps, proj, outer, back, inner,
          velocity, mixing_local, active)
    return (state.reshape(comps, rows, width), velocity.reshape(ocean_vel.shape))


def solution(mesh):
    placed = (
        P("spec", "space", None),
        P("space", None),
        P(),
        P(),
        P(),
        P(None, None, "spec", "space", None),
        P(None, "spec", "space", None),
        P("spec", "space", None),
    )
    return jax.shard_map(
        body,
        mesh=mesh,
        in_specs=placed,
        out_specs=(P("spec", "space", None), P(None, None, "spec", "space", None)),
        check_vma=False,
    )
```

```python
import functools
import math

import jax
import jax.numpy as jnp
import numpy as np
from jax import lax
from jax.experimental import pallas as pl
from jax.experimental.pallas import tpu as pltpu
from jax.sharding import PartitionSpec as P

NDIR = 36
NFREQ = 36
K = NDIR * NFREQ
STEPS = 2

courant_scale = 0.5
current_scale = 0.15
source_step = 0.25
coriolis = 0.3
stress_scale = 0.5
drift_scale = 4.0

MESH = pl.DeviceIdType.MESH
F32 = jnp.float32
BF16 = jnp.bfloat16
VMEM_LIMIT = 60 * 1024 * 1024
ROWS = 16


def tap_table():
    component = np.arange(K)
    frequency = component // NDIR
    direction = component % NDIR
    angle = (direction + 0.5) * (2.0 * math.pi / NDIR)
    speed = courant_scale * np.exp(-2.0 * frequency / NFREQ)
    eastward = (4 * direction + 2 < NDIR) | (4 * direction + 2 > 3 * NDIR)
    northward = 2 * direction + 1 < NDIR
    forward = (1.0 / 6.0, -1.0, 0.5, 2.0 / 6.0, 0.0)
    backward = (0.0, -2.0 / 6.0, -0.5, 1.0, -1.0 / 6.0)
    columns = [speed * np.cos(angle), speed * np.sin(angle)]
    for mask in (eastward, northward):
        for f, b in zip(forward, backward):
            columns.append(np.where(mask, f, b))
    return np.stack(columns, 1).astype(np.float32)


def coupling_tables(layers):
    component = np.arange(K)
    frequency = component // NDIR
    angle = (component % NDIR + 0.5) * (2.0 * math.pi / NDIR)
    wavenum = 0.02 * np.exp(6.0 * frequency / NFREQ)
    depth = np.arange(layers)[:, None] + 0.5
    decay_rows = wavenum[None, :] ** 1.5 * np.exp(-2.0 * wavenum[None, :] * depth)
    decay_rows = decay_rows / np.sqrt(np.sum(decay_rows * decay_rows, axis=1, keepdims=True))
    drift_rows = drift_scale * np.concatenate(
        [decay_rows * np.cos(angle)[None, :], decay_rows * np.sin(angle)[None, :]], 0
    )
    stress = wavenum / np.sqrt(np.sum(wavenum * wavenum))
    stress_rows = -stress_scale * np.stack([stress * np.cos(angle), stress * np.sin(angle)], 0)
    return (drift_rows.astype(np.float32), stress_rows.astype(np.float32))


def pieces(rows):
    first = lax.reduce_precision(rows, 8, 7)
    rest = rows - first
    second = lax.reduce_precision(rest, 8, 7)
    third = rest - second
    return jnp.concatenate([first, second, third], 0).astype(BF16)


def constant_pieces(rows):
    first = rows.astype(BF16)
    rest = rows - first.astype(np.float32)
    second = rest.astype(BF16)
    third = (rest - second.astype(np.float32)).astype(BF16)
    return np.concatenate([first, second, third], 0)


def step_kernel(
    width, owners, inverse, state, land, place, rank, my_rank, taps, proj, outer, back, inner, velocity, mixing, active,
    out, new_velocity,
    field, east, north, drift, blocks, got, made, returned, stage, pay, surface, surfaces,
    head, tail, before, after, east_head, east_tail, east_before, east_after,
    send_in, recv_in, send_back, recv_back, send_top, recv_top, send_edge, recv_edge,
    *relay
):
    slots, chunks, comps, chunk_width = blocks.shape
    padded = field.shape[1]
    points = state.shape[1]
    block = points // slots
    block_rows = block // width
    rank_rows = back.shape[2]
    layers = mixing.shape[0]
    me = lax.axis_index("spec")
    strip = lax.axis_index("space")
    strips = lax.axis_size("space")
    edge = 2 * width
    has_before = strip > 0
    has_after = strip < strips - 1

    def peer(delta):
        return lax.rem(me + delta, slots)

    def spread_out(target, rows_at, low, value):
        for b in range(slots):
            start, stop = b * block, (b + 1) * block + 2 * edge
            first, last = max(start, low), min(stop, low + value.shape[1])
            if first < last:
                target[b, rows_at, first - start : last - start] = value[:, first - low : last - low]

    def copy(source, target, send, receive, device):
        return pltpu.make_async_remote_copy(
            src_ref=source, dst_ref=target, send_sem=send, recv_sem=receive,
            device_id=device, device_id_type=MESH,
        )

    def inward(j, delta):
        return copy(
            blocks.at[peer(delta), j], got.at[j, me],
            send_in.at[j, delta], recv_in.at[j, delta], {"spec": peer(delta)},
        )

    def homeward(j, delta):
        return copy(
            made.at[j, peer(delta)], returned.at[j, me],
            send_back.at[j, delta], recv_back.at[j, delta], {"spec": peer(delta)},
        )

    if relay:
        (cube, cubes, moved, landed, send_cube, recv_cube, send_moved, recv_moved) = relay
        half = me // 2
        mate = me + 1 - 2 * (me % 2)
        other = 2 - 2 * half
        hub = 2 - half
        inner_device = (me == 1) | (me == 2)

    def to_mate(j):
        return copy(
            made.at[j, mate], returned.at[j, me],
            send_back.at[j, 0], recv_back.at[j, 0], {"spec": mate},
        )

    def to_hub(j):
        return copy(
            cube.at[j], cubes.at[j, me % 2],
            send_cube.at[j], recv_cube.at[j, me % 2], {"spec": hub},
        )

    def from_owner(j, k):
        return copy(cube.at[j], cubes.at[j, k], send_cube.at[j], recv_cube.at[j, k], {"spec": hub})

    def onward(j, k):
        return copy(
            moved.at[j, k], landed.at[j, k],
            send_moved.at[j, k], recv_moved.at[j, k], {"spec": mate},
        )

    def pass_on(j):
        for k in range(2):
            from_owner(j, k).wait_recv()
            moved[j, k] = jnp.dot(
                back[mate], cubes[j, k], preferred_element_type=F32
            ).astype(BF16)
            onward(j, k).start()
        for k in range(2):
            transfer = jnp.dot(back[me], cubes[j, k], preferred_element_type=F32)
            returned[j, other + k] = (
                blocks[other + k, j].astype(F32) + source_step * transfer
            ).astype(BF16)

    def take_in(j):
        for k in range(2):
            onward(j, k).wait_recv()
            returned[j, other + k] = (
                blocks[other + k, j].astype(F32) + source_step * landed[j, k].astype(F32)
            ).astype(BF16)

    def upward(delta):
        return copy(
            surface, surfaces.at[me], send_top.at[delta], recv_top.at[delta], {"spec": peer(delta)}
        )

    def to_before(source, target, i):
        return copy(source, target, send_edge.at[i], recv_edge.at[i], {"space": strip - 1})

    def to_after(source, target, i):
        return copy(source, target, send_edge.at[i], recv_edge.at[i], {"space": strip + 1})

    barrier = pltpu.get_barrier_semaphore()
    for delta in range(1, slots):
        pl.semaphore_signal(
            barrier, inc=1, device_id={"spec": peer(delta)}, device_id_type=MESH
        )

    @pl.when(has_before)
    def _():
        pl.semaphore_signal(barrier, inc=1, device_id={"space": strip - 1}, device_id_type=MESH)

    @pl.when(has_after)
    def _():
        pl.semaphore_signal(barrier, inc=1, device_id={"space": strip + 1}, device_id_type=MESH)

    surface[0:1, :] = velocity[0, 0:1, :]
    surface[1:2, :] = velocity[1, 0:1, :]
    everywhere = jnp.concatenate([land[b] for b in range(slots)], 1)
    head[...] = (state[:, :edge].astype(F32) * everywhere[:, :edge]).astype(BF16)
    tail[...] = (state[:, points - edge :].astype(F32) * everywhere[:, points - edge :]).astype(BF16)
    expected = slots - 1 + has_before.astype(jnp.int32) + has_after.astype(jnp.int32)
    pl.semaphore_wait(barrier, expected)

    for delta in range(1, slots):
        upward(delta).start()

    @pl.when(has_before)
    def _():
        to_before(head, after, 0).start()

    @pl.when(has_after)
    def _():
        to_after(tail, before, 1).start()

    surfaces[me] = surface[...]
    whole_chunks = comps // ROWS
    rest = comps - whole_chunks * ROWS

    def fill(index, carry):
        here = pl.ds(pl.multiple_of(index * ROWS, ROWS), ROWS)
        masked = (state[here, :].astype(F32) * everywhere).astype(BF16)
        spread_out(field, here, edge, masked)
        return carry

    lax.fori_loop(0, whole_chunks, fill, 0)
    if rest:
        at = whole_chunks * ROWS
        for b in range(slots):
            field[b, at:, :] = jnp.zeros((padded - at, field.shape[2]), BF16)
        masked = (state[at:, :].astype(F32) * everywhere).astype(BF16)
        spread_out(field, slice(at, comps), edge, masked)

    for delta in range(1, slots):
        upward(delta).wait()
    currents = []
    for b in range(slots):
        here = jnp.zeros((2, block), F32)
        for s in range(slots):
            here = here + place[b, s] * surfaces[s]
        currents.append(here)
        north[b] = here[1:2]
    eastward = jnp.concatenate([here[0:1] for here in currents], 1)
    spread_out(east, slice(0, 1), edge, eastward)
    east_head[...] = eastward[:, :edge]
    east_tail[...] = eastward[:, points - edge :]

    @pl.when(has_before)
    def _():
        to_before(east_head, east_after, 2).start()

    @pl.when(has_after)
    def _():
        to_after(east_tail, east_before, 3).start()

    @pl.when(has_after)
    def _():
        to_after(head, after, 0).wait_recv()
        to_after(east_head, east_after, 2).wait_recv()
        spread_out(field, slice(0, comps), edge + points, after[...])
        spread_out(east, slice(0, 1), edge + points, east_after[...])

    @pl.when(jnp.logical_not(has_after))
    def _():
        spread_out(field, slice(0, comps), edge + points, jnp.zeros((comps, edge), BF16))
        spread_out(east, slice(0, 1), edge + points, jnp.zeros((1, edge), F32))

    @pl.when(has_before)
    def _():
        to_before(tail, before, 1).wait_recv()
        to_before(east_tail, east_before, 3).wait_recv()
        spread_out(field, slice(0, comps), 0, before[...])
        spread_out(east, slice(0, 1), 0, east_before[...])

    @pl.when(jnp.logical_not(has_before))
    def _():
        spread_out(field, slice(0, comps), 0, jnp.zeros((comps, edge), BF16))
        spread_out(east, slice(0, 1), 0, jnp.zeros((1, edge), F32))

    column = lax.broadcasted_iota(jnp.int32, (ROWS, width), 1)
    position = lax.broadcasted_iota(jnp.int32, (chunks * chunk_width, block), 0)

    def shifted(value, by):
        turned = pltpu.roll(value, by % width, 1)
        inside = (column >= by) if by > 0 else (column < width + by)
        return jnp.where(inside, turned, 0.0)

    def advect(b):
        def lanes(r):
            return slice(r * width, (r + 1) * width)

        def chunk(index, carry):
            here = pl.ds(pl.multiple_of(index * ROWS, ROWS), ROWS)
            tap = taps[here, :]

            def spread(i):
                return jnp.broadcast_to(tap[:, i : i + 1], (ROWS, width))

            speed_east, speed_north = spread(0), spread(1)
            row_tap = [spread(2 + i) for i in range(5)]
            col_tap = [spread(7 + i) for i in range(5)]
            masked = {}
            flow = {}
            for r in range(-2, block_rows + 2):
                masked[r] = field[b, here, lanes(r + 2)].astype(F32)
                flow[r] = (speed_east + current_scale * east[b, :, lanes(r + 2)]) * masked[r]
                c = r - 2
                if c < 0:
                    continue
                m = masked.pop(c)
                along = (speed_north + current_scale * north[b, :, lanes(c)]) * m
                total = m
                for i in range(5):
                    total = total - row_tap[i] * flow[c - 2 + i]
                total = total - col_tap[2] * along
                for i in (0, 1, 3, 4):
                    total = total - col_tap[i] * shifted(along, 2 - i)
                flow.pop(c - 2)
                drift[here, c * width : (c + 1) * width] = (total * land[b, :, lanes(c)]).astype(BF16)
            return carry

        lax.fori_loop(0, padded // ROWS, chunk, 0)
        spot = (position == rank[b]).astype(F32).astype(BF16)
        return lax.dot_general(
            drift[...], spot, (((1,), (1,)), ((), ())), preferred_element_type=F32
        ).astype(BF16)

    def one_slot(delta, carry):
        slot = peer(delta)
        packed = advect(owners[slot])

        for j in range(chunks):
            part = packed[:comps, j * chunk_width : (j + 1) * chunk_width]
            blocks[slot, j] = part

        @pl.when(delta < slots)
        def _():
            for j in range(chunks):
                inward(j, delta).start()

        return carry

    lax.fori_loop(1, slots + 1, one_slot, 0)
    for j in range(chunks):
        got[j, me] = blocks[me, j]

    def one_chunk(j, carry):
        for delta in range(1, slots):
            inward(j, delta).wait_recv()
        projected = jnp.dot(proj[0], got[j, 0], preferred_element_type=F32)
        for g in range(1, slots):
            projected = projected + jnp.dot(proj[g], got[j, g], preferred_element_type=F32)
        cubed = (projected * projected * projected).astype(BF16)
        if relay:
            cube[j] = cubed
            to_hub(j).start()
            targets = [(mate, 1), (me, 0)]
        else:
            targets = [(peer(delta), delta) for delta in list(range(1, slots)) + [0]]
        for g, delta in targets:
            transfer = jnp.dot(back[g], cubed, preferred_element_type=F32)
            updated = (got[j, g].astype(F32) + source_step * transfer).astype(BF16)
            if delta:
                made[j, g] = updated
                (to_mate(j) if relay else homeward(j, delta)).start()
            else:
                returned[j, g] = updated
        more = jnp.dot(inner[...], cubed, preferred_element_type=F32)
        for g in range(slots):
            more = more + jnp.dot(outer[g], got[j, g], preferred_element_type=F32)
        third = more.shape[0] // 3
        pay[j] = more[:third] + more[third : 2 * third] + more[2 * third :]
        if relay:

            @pl.when(inner_device & (j > 0))
            def _():
                pass_on(jnp.maximum(j - 1, 0))

        return carry

    lax.fori_loop(0, chunks, one_chunk, 0)
    if relay:

        @pl.when(inner_device)
        def _():
            pass_on(chunks - 1)


    payload = None
    for j in range(chunks):
        spot = lax.broadcasted_iota(jnp.int32, (chunk_width, block), 0) + j * chunk_width
        spot = (spot == my_rank[...]).astype(F32).astype(BF16)
        value = pay[j]
        for _ in range(3):
            part = value.astype(BF16)
            value = value - part.astype(F32)
            term = jnp.dot(part, spot, preferred_element_type=F32)
            payload = term if payload is None else payload + term

    layer = lax.broadcasted_iota(jnp.int32, (layers, block), 0)
    depth = active[...]
    live = (layer < depth).astype(F32)
    bottom = (layer == depth - 1).astype(F32)
    top = (layer == 0).astype(F32)
    mix = mixing[...]
    upper = mix * ((layer + 1 < depth) & (layer < layers - 1)).astype(F32)

    def mixed(value):
        between = upper * (value - pltpu.roll(value, layers - 1, 0))
        return pltpu.roll(between, 1, 0) - between - mix * bottom * value

    old_east, old_north = velocity[0], velocity[1]
    drift_east = payload[:layers]
    drift_north = payload[layers : 2 * layers]
    stress_east = payload[2 * layers : 2 * layers + 1]
    stress_north = payload[2 * layers + 1 : 2 * layers + 2]
    new_velocity[0] = live * (
        old_east + coriolis * (old_north + drift_north) + mixed(old_east) + top * stress_east
    )
    new_velocity[1] = live * (
        old_north - coriolis * (old_east + drift_east) + mixed(old_north) + top * stress_north
    )

    def expand(j, carry):
        if relay:
            to_mate(j).wait_recv()

            @pl.when(jnp.logical_not(inner_device))
            def _():
                take_in(j)

        else:
            for delta in range(1, slots):
                homeward(j, delta).wait_recv()
        for s in range(slots):
            stage[s] = returned[j, s]
        spot = lax.broadcasted_iota(jnp.int32, (chunk_width, block), 0) + j * chunk_width
        for b in range(slots):
            at = slice(b * block, (b + 1) * block)
            here = (spot == rank[b]).astype(F32).astype(BF16)
            term = jnp.dot(
                stage[inverse[b]], here, preferred_element_type=F32
            ).astype(BF16)

            @pl.when(j == 0)
            def _():
                out[:, at] = term

            @pl.when(j > 0)
            def _():
                out[:, at] = out[:, at] + term

        return carry

    lax.fori_loop(0, chunks, expand, 0)

    @pl.when(has_before)
    def _():
        to_before(head, after, 0).wait_send()
        to_before(east_head, east_after, 2).wait_send()

    @pl.when(has_after)
    def _():
        to_after(tail, before, 1).wait_send()
        to_after(east_tail, east_before, 3).wait_send()

    for j in range(chunks):
        for delta in range(1, slots):
            inward(j, delta).wait_send()
            if not relay:
                homeward(j, delta).wait_send()
        if relay:
            to_mate(j).wait_send()
            to_hub(j).wait_send()
    if relay:

        @pl.when(inner_device)
        def _():
            for j in range(chunks):
                for k in range(2):
                    onward(j, k).wait_send()


def whole(count, memory=pltpu.VMEM):
    return [pl.BlockSpec(memory_space=memory)] * count


def body(spectrum, land_sea, owners, proj_weight, back_weight, ocean_vel, mixing, active_layers):
    comps, rows, width = spectrum.shape
    slots = lax.axis_size("spec")
    points = rows * width
    block = points // slots
    cap = block * 3 // 4
    chunk_width = 256 if cap % 256 == 0 else cap
    chunks = cap // chunk_width
    layers = mixing.shape[0]
    rank_rows = proj_weight.shape[0]
    padded = -(-comps // ROWS) * ROWS
    edge = 2 * width
    me = lax.axis_index("spec")

    table = np.zeros((slots, padded, 12), np.float32)
    table[:, :comps] = tap_table().reshape(slots, comps, 12)
    taps = lax.dynamic_index_in_dim(jnp.asarray(table), me, 0, False)
    drift_rows, stress_rows = coupling_tables(layers)
    zeros = np.zeros((6, K), np.float32)
    outer = constant_pieces(np.concatenate([drift_rows, zeros, zeros[:2]], 0))
    outer = jnp.asarray(
        np.ascontiguousarray(outer.reshape(outer.shape[0], slots, comps).transpose(1, 0, 2))
    )
    through = jnp.dot(
        jnp.asarray(np.concatenate([source_step * drift_rows, stress_rows, zeros], 0)),
        back_weight.astype(F32),
        precision=lax.Precision.HIGHEST,
    )
    inner = pieces(through)
    proj = jnp.transpose(proj_weight.reshape(rank_rows, slots, comps), (1, 0, 2))
    back = back_weight.reshape(slots, comps, rank_rows)

    land = land_sea.astype(F32).reshape(slots, 1, block)
    covers = (owners[None, :] == jnp.arange(slots, dtype=jnp.int32)[:, None]).astype(jnp.int32)
    inverse = jnp.sum(covers * jnp.arange(slots, dtype=jnp.int32)[None], 1)
    place = jnp.broadcast_to(covers.astype(F32)[:, :, None, None], (slots, slots, 1, block))
    sea = land_sea.reshape(slots, block)
    rank = jnp.where(sea > 0, jnp.cumsum(sea, 1) - 1, -1).reshape(slots, 1, block)
    my_rank = lax.dynamic_index_in_dim(rank, owners[me], 0, False)

    velocity = ocean_vel.reshape(2, layers, block)
    mixing_local = mixing.reshape(layers, block)
    active = active_layers.reshape(1, block)
    state = spectrum.reshape(comps, points)
    pay_rows = inner.shape[0] // 3
    exchange = pltpu.VMEM((chunks, slots, comps, chunk_width), BF16)
    relay = []
    if slots == 4:
        pair = pltpu.VMEM((chunks, 2, comps, chunk_width), BF16)
        both = pltpu.SemaphoreType.DMA((chunks, 2))
        relay = [
            pltpu.VMEM((chunks, rank_rows, chunk_width), BF16),
            pltpu.VMEM((chunks, 2, rank_rows, chunk_width), BF16),
            pair, pair, pltpu.SemaphoreType.DMA((chunks,)), both, both, both,
        ]
    for _ in range(STEPS):
        state, velocity = pl.pallas_call(
            functools.partial(step_kernel, width),
            out_shape=(
                jax.ShapeDtypeStruct((comps, points), BF16),
                jax.ShapeDtypeStruct((2, layers, block), F32),
            ),
            in_specs=whole(2, pltpu.SMEM) + whole(13),
            out_specs=tuple(whole(2)),
            scratch_shapes=[
                pltpu.VMEM((slots, padded, block + 2 * edge), BF16),
                pltpu.VMEM((slots, 1, block + 2 * edge), F32),
                pltpu.VMEM((slots, 1, block), F32),
                pltpu.VMEM((padded, block), BF16),
                pltpu.VMEM((slots, chunks, comps, chunk_width), BF16),
                exchange,
                exchange,
                exchange,
                pltpu.VMEM((slots, comps, chunk_width), BF16),
                pltpu.VMEM((chunks, pay_rows, chunk_width), F32),
                pltpu.VMEM((2, block), F32),
                pltpu.VMEM((slots, 2, block), F32),
            ]
            + [pltpu.VMEM((comps, edge), BF16)] * 4
            + [pltpu.VMEM((1, edge), F32)] * 4
            + [pltpu.SemaphoreType.DMA((chunks, slots))] * 4
            + [pltpu.SemaphoreType.DMA((slots,))] * 2
            + [pltpu.SemaphoreType.DMA((4,))] * 2
            + relay,
            compiler_params=pltpu.CompilerParams(
                vmem_limit_bytes=VMEM_LIMIT, collective_id=0, has_side_effects=True
            ),
            name="step",
        )(owners, inverse, state, land, place, rank, my_rank, taps, proj, outer, back, inner,
          velocity, mixing_local, active)
    return (state.reshape(comps, rows, width), velocity.reshape(ocean_vel.shape))


def solution(mesh):
    placed = (
        P("spec", "space", None),
        P("space", None),
        P(),
        P(),
        P(),
        P(None, None, "spec", "space", None),
        P(None, "spec", "space", None),
        P("spec", "space", None),
    )
    return jax.shard_map(
        body,
        mesh=mesh,
        in_specs=placed,
        out_specs=(P("spec", "space", None), P(None, None, "spec", "space", None)),
        check_vma=False,
    )
```

```python
import functools
import math

import jax
import jax.numpy as jnp
import numpy as np
from jax import lax
from jax.experimental import pallas as pl
from jax.experimental.pallas import tpu as pltpu
from jax.sharding import PartitionSpec as P

NDIR = 36
NFREQ = 36
K = NDIR * NFREQ
STEPS = 2

courant_scale = 0.5
current_scale = 0.15
source_step = 0.25
coriolis = 0.3
stress_scale = 0.5
drift_scale = 4.0

MESH = pl.DeviceIdType.MESH
F32 = jnp.float32
BF16 = jnp.bfloat16
VMEM_LIMIT = 60 * 1024 * 1024
ROWS = 16


def tap_table():
    component = np.arange(K)
    frequency = component // NDIR
    direction = component % NDIR
    angle = (direction + 0.5) * (2.0 * math.pi / NDIR)
    speed = courant_scale * np.exp(-2.0 * frequency / NFREQ)
    eastward = (4 * direction + 2 < NDIR) | (4 * direction + 2 > 3 * NDIR)
    northward = 2 * direction + 1 < NDIR
    forward = (1.0 / 6.0, -1.0, 0.5, 2.0 / 6.0, 0.0)
    backward = (0.0, -2.0 / 6.0, -0.5, 1.0, -1.0 / 6.0)
    columns = [speed * np.cos(angle), speed * np.sin(angle)]
    for mask in (eastward, northward):
        for f, b in zip(forward, backward):
            columns.append(np.where(mask, f, b))
    return np.stack(columns, 1).astype(np.float32)


def coupling_tables(layers):
    component = np.arange(K)
    frequency = component // NDIR
    angle = (component % NDIR + 0.5) * (2.0 * math.pi / NDIR)
    wavenum = 0.02 * np.exp(6.0 * frequency / NFREQ)
    depth = np.arange(layers)[:, None] + 0.5
    decay_rows = wavenum[None, :] ** 1.5 * np.exp(-2.0 * wavenum[None, :] * depth)
    decay_rows = decay_rows / np.sqrt(np.sum(decay_rows * decay_rows, axis=1, keepdims=True))
    drift_rows = drift_scale * np.concatenate(
        [decay_rows * np.cos(angle)[None, :], decay_rows * np.sin(angle)[None, :]], 0
    )
    stress = wavenum / np.sqrt(np.sum(wavenum * wavenum))
    stress_rows = -stress_scale * np.stack([stress * np.cos(angle), stress * np.sin(angle)], 0)
    return (drift_rows.astype(np.float32), stress_rows.astype(np.float32))


def pieces(rows):
    first = lax.reduce_precision(rows, 8, 7)
    rest = rows - first
    second = lax.reduce_precision(rest, 8, 7)
    third = rest - second
    return jnp.concatenate([first, second, third], 0).astype(BF16)


def constant_pieces(rows):
    first = rows.astype(BF16)
    rest = rows - first.astype(np.float32)
    second = rest.astype(BF16)
    third = (rest - second.astype(np.float32)).astype(BF16)
    return np.concatenate([first, second, third], 0)


def step_kernel(
    width, owners, inverse, state, land, place, rank, my_rank, taps, proj, outer, back, inner, velocity, mixing, active,
    out, new_velocity,
    field, east, north, drift, blocks, got, made, returned, stage, pay, surface, surfaces,
    head, tail, before, after, east_head, east_tail, east_before, east_after,
    send_in, recv_in, send_back, recv_back, send_top, recv_top, send_edge, recv_edge,
    *relay
):
    slots, chunks, comps, chunk_width = blocks.shape
    padded = field.shape[1]
    points = state.shape[1]
    block = points // slots
    block_rows = block // width
    rank_rows = back.shape[2]
    layers = mixing.shape[0]
    me = lax.axis_index("spec")
    strip = lax.axis_index("space")
    strips = lax.axis_size("space")
    edge = 2 * width
    has_before = strip > 0
    has_after = strip < strips - 1

    def peer(delta):
        return lax.rem(me + delta, slots)

    def spread_out(target, rows_at, low, value):
        for b in range(slots):
            start, stop = b * block, (b + 1) * block + 2 * edge
            first, last = max(start, low), min(stop, low + value.shape[1])
            if first < last:
                target[b, rows_at, first - start : last - start] = value[:, first - low : last - low]

    def copy(source, target, send, receive, device):
        return pltpu.make_async_remote_copy(
            src_ref=source, dst_ref=target, send_sem=send, recv_sem=receive,
            device_id=device, device_id_type=MESH,
        )

    def inward(j, delta):
        return copy(
            blocks.at[peer(delta), j], got.at[j, me],
            send_in.at[j, delta], recv_in.at[j, delta], {"spec": peer(delta)},
        )

    def homeward(j, delta):
        return copy(
            made.at[j, peer(delta)], returned.at[j, me],
            send_back.at[j, delta], recv_back.at[j, delta], {"spec": peer(delta)},
        )

    if relay:
        (cube, cubes, moved, landed, send_cube, recv_cube, send_moved, recv_moved) = relay
        half = me // 2
        mate = me + 1 - 2 * (me % 2)
        other = 2 - 2 * half
        hub = 2 - half
        inner_device = (me == 1) | (me == 2)

    def to_mate(j):
        return copy(
            made.at[j, mate], returned.at[j, me],
            send_back.at[j, 0], recv_back.at[j, 0], {"spec": mate},
        )

    def to_hub(j):
        return copy(
            cube.at[j], cubes.at[j, me % 2],
            send_cube.at[j], recv_cube.at[j, me % 2], {"spec": hub},
        )

    def from_owner(j, k):
        return copy(cube.at[j], cubes.at[j, k], send_cube.at[j], recv_cube.at[j, k], {"spec": hub})

    def onward(j, k):
        return copy(
            moved.at[j, k], landed.at[j, k],
            send_moved.at[j, k], recv_moved.at[j, k], {"spec": mate},
        )

    def pass_on(j):
        for k in range(2):
            from_owner(j, k).wait_recv()
            moved[j, k] = jnp.dot(
                back[mate], cubes[j, k], preferred_element_type=F32
            ).astype(BF16)
            onward(j, k).start()
        for k in range(2):
            transfer = jnp.dot(back[me], cubes[j, k], preferred_element_type=F32)
            returned[j, other + k] = (
                blocks[other + k, j].astype(F32) + source_step * transfer
            ).astype(BF16)

    def take_in(j):
        for k in range(2):
            onward(j, k).wait_recv()
            returned[j, other + k] = (
                blocks[other + k, j].astype(F32) + source_step * landed[j, k].astype(F32)
            ).astype(BF16)

    def upward(delta):
        return copy(
            surface, surfaces.at[me], send_top.at[delta], recv_top.at[delta], {"spec": peer(delta)}
        )

    def to_before(source, target, i):
        return copy(source, target, send_edge.at[i], recv_edge.at[i], {"space": strip - 1})

    def to_after(source, target, i):
        return copy(source, target, send_edge.at[i], recv_edge.at[i], {"space": strip + 1})

    barrier = pltpu.get_barrier_semaphore()
    for delta in range(1, slots):
        pl.semaphore_signal(
            barrier, inc=1, device_id={"spec": peer(delta)}, device_id_type=MESH
        )

    @pl.when(has_before)
    def _():
        pl.semaphore_signal(barrier, inc=1, device_id={"space": strip - 1}, device_id_type=MESH)

    @pl.when(has_after)
    def _():
        pl.semaphore_signal(barrier, inc=1, device_id={"space": strip + 1}, device_id_type=MESH)

    surface[0:1, :] = velocity[0, 0:1, :]
    surface[1:2, :] = velocity[1, 0:1, :]
    everywhere = jnp.concatenate([land[b] for b in range(slots)], 1)
    head[...] = (state[:, :edge].astype(F32) * everywhere[:, :edge]).astype(BF16)
    tail[...] = (state[:, points - edge :].astype(F32) * everywhere[:, points - edge :]).astype(BF16)
    expected = slots - 1 + has_before.astype(jnp.int32) + has_after.astype(jnp.int32)
    pl.semaphore_wait(barrier, expected)

    for delta in range(1, slots):
        upward(delta).start()

    @pl.when(has_before)
    def _():
        to_before(head, after, 0).start()

    @pl.when(has_after)
    def _():
        to_after(tail, before, 1).start()

    surfaces[me] = surface[...]
    whole_chunks = comps // ROWS
    rest = comps - whole_chunks * ROWS

    def fill(index, carry):
        here = pl.ds(pl.multiple_of(index * ROWS, ROWS), ROWS)
        masked = (state[here, :].astype(F32) * everywhere).astype(BF16)
        spread_out(field, here, edge, masked)
        return carry

    lax.fori_loop(0, whole_chunks, fill, 0)
    if rest:
        at = whole_chunks * ROWS
        for b in range(slots):
            field[b, at:, :] = jnp.zeros((padded - at, field.shape[2]), BF16)
        masked = (state[at:, :].astype(F32) * everywhere).astype(BF16)
        spread_out(field, slice(at, comps), edge, masked)

    for delta in range(1, slots):
        upward(delta).wait()
    currents = []
    for b in range(slots):
        here = jnp.zeros((2, block), F32)
        for s in range(slots):
            here = here + place[b, s] * surfaces[s]
        currents.append(here)
        north[b] = here[1:2]
    eastward = jnp.concatenate([here[0:1] for here in currents], 1)
    spread_out(east, slice(0, 1), edge, eastward)
    east_head[...] = eastward[:, :edge]
    east_tail[...] = eastward[:, points - edge :]

    @pl.when(has_before)
    def _():
        to_before(east_head, east_after, 2).start()

    @pl.when(has_after)
    def _():
        to_after(east_tail, east_before, 3).start()

    @pl.when(has_after)
    def _():
        to_after(head, after, 0).wait_recv()
        to_after(east_head, east_after, 2).wait_recv()
        spread_out(field, slice(0, comps), edge + points, after[...])
        spread_out(east, slice(0, 1), edge + points, east_after[...])

    @pl.when(jnp.logical_not(has_after))
    def _():
        spread_out(field, slice(0, comps), edge + points, jnp.zeros((comps, edge), BF16))
        spread_out(east, slice(0, 1), edge + points, jnp.zeros((1, edge), F32))

    @pl.when(has_before)
    def _():
        to_before(tail, before, 1).wait_recv()
        to_before(east_tail, east_before, 3).wait_recv()
        spread_out(field, slice(0, comps), 0, before[...])
        spread_out(east, slice(0, 1), 0, east_before[...])

    @pl.when(jnp.logical_not(has_before))
    def _():
        spread_out(field, slice(0, comps), 0, jnp.zeros((comps, edge), BF16))
        spread_out(east, slice(0, 1), 0, jnp.zeros((1, edge), F32))

    column = lax.broadcasted_iota(jnp.int32, (ROWS, width), 1)
    position = lax.broadcasted_iota(jnp.int32, (chunks * chunk_width, block), 0)

    def shifted(value, by):
        turned = pltpu.roll(value, by % width, 1)
        inside = (column >= by) if by > 0 else (column < width + by)
        return jnp.where(inside, turned, 0.0)

    def advect(b):
        def lanes(r):
            return slice(r * width, (r + 1) * width)

        def chunk(index, carry):
            here = pl.ds(pl.multiple_of(index * ROWS, ROWS), ROWS)
            tap = taps[here, :]

            def spread(i):
                return jnp.broadcast_to(tap[:, i : i + 1], (ROWS, width))

            speed_east, speed_north = spread(0), spread(1)
            row_tap = [spread(2 + i) for i in range(5)]
            col_tap = [spread(7 + i) for i in range(5)]
            masked = {}
            flow = {}
            for r in range(-2, block_rows + 2):
                masked[r] = field[b, here, lanes(r + 2)].astype(F32)
                flow[r] = (speed_east + current_scale * east[b, :, lanes(r + 2)]) * masked[r]
                c = r - 2
                if c < 0:
                    continue
                m = masked.pop(c)
                along = (speed_north + current_scale * north[b, :, lanes(c)]) * m
                total = m
                for i in range(5):
                    total = total - row_tap[i] * flow[c - 2 + i]
                total = total - col_tap[2] * along
                for i in (0, 1, 3, 4):
                    total = total - col_tap[i] * shifted(along, 2 - i)
                flow.pop(c - 2)
                drift[here, c * width : (c + 1) * width] = (total * land[b, :, lanes(c)]).astype(BF16)
            return carry

        lax.fori_loop(0, padded // ROWS, chunk, 0)
        spot = (position == rank[b]).astype(F32).astype(BF16)
        return lax.dot_general(
            drift[...], spot, (((1,), (1,)), ((), ())), preferred_element_type=F32
        ).astype(BF16)

    def one_slot(delta, carry):
        slot = peer(delta)
        packed = advect(owners[slot])

        for j in range(chunks):
            part = packed[:comps, j * chunk_width : (j + 1) * chunk_width]
            blocks[slot, j] = part

        @pl.when(delta < slots)
        def _():
            for j in range(chunks):
                inward(j, delta).start()

        return carry

    lax.fori_loop(1, slots + 1, one_slot, 0)
    for j in range(chunks):
        got[j, me] = blocks[me, j]

    def one_chunk(j, carry):
        for delta in range(1, slots):
            inward(j, delta).wait_recv()
        projected = jnp.dot(proj[0], got[j, 0], preferred_element_type=F32)
        for g in range(1, slots):
            projected = projected + jnp.dot(proj[g], got[j, g], preferred_element_type=F32)
        cubed = (projected * projected * projected).astype(BF16)
        if relay:
            cube[j] = cubed
            to_hub(j).start()
            targets = [(mate, 1), (me, 0)]
        else:
            targets = [(peer(delta), delta) for delta in list(range(1, slots)) + [0]]
        for g, delta in targets:
            transfer = jnp.dot(back[g], cubed, preferred_element_type=F32)
            updated = (got[j, g].astype(F32) + source_step * transfer).astype(BF16)
            if delta:
                made[j, g] = updated
                (to_mate(j) if relay else homeward(j, delta)).start()
            else:
                returned[j, g] = updated
        more = jnp.dot(inner[...], cubed, preferred_element_type=F32)
        for g in range(slots):
            more = more + jnp.dot(outer[g], got[j, g], preferred_element_type=F32)
        third = more.shape[0] // 3
        pay[j] = more[:third] + more[third : 2 * third] + more[2 * third :]
        if relay:

            @pl.when(inner_device & (j > 0))
            def _():
                pass_on(jnp.maximum(j - 1, 0))

        return carry

    lax.fori_loop(0, chunks, one_chunk, 0)
    if relay:

        @pl.when(inner_device)
        def _():
            pass_on(chunks - 1)


    payload = None
    for j in range(chunks):
        spot = lax.broadcasted_iota(jnp.int32, (chunk_width, block), 0) + j * chunk_width
        spot = (spot == my_rank[...]).astype(F32).astype(BF16)
        value = pay[j]
        for _ in range(3):
            part = value.astype(BF16)
            value = value - part.astype(F32)
            term = jnp.dot(part, spot, preferred_element_type=F32)
            payload = term if payload is None else payload + term

    layer = lax.broadcasted_iota(jnp.int32, (layers, block), 0)
    depth = active[...]
    live = (layer < depth).astype(F32)
    bottom = (layer == depth - 1).astype(F32)
    top = (layer == 0).astype(F32)
    mix = mixing[...]
    upper = mix * ((layer + 1 < depth) & (layer < layers - 1)).astype(F32)

    def mixed(value):
        between = upper * (value - pltpu.roll(value, layers - 1, 0))
        return pltpu.roll(between, 1, 0) - between - mix * bottom * value

    old_east, old_north = velocity[0], velocity[1]
    drift_east = payload[:layers]
    drift_north = payload[layers : 2 * layers]
    stress_east = payload[2 * layers : 2 * layers + 1]
    stress_north = payload[2 * layers + 1 : 2 * layers + 2]
    new_velocity[0] = live * (
        old_east + coriolis * (old_north + drift_north) + mixed(old_east) + top * stress_east
    )
    new_velocity[1] = live * (
        old_north - coriolis * (old_east + drift_east) + mixed(old_north) + top * stress_north
    )

    def expand(j, carry):
        if relay:
            to_mate(j).wait_recv()

            @pl.when(jnp.logical_not(inner_device))
            def _():
                take_in(j)

        else:
            for delta in range(1, slots):
                homeward(j, delta).wait_recv()
        for s in range(slots):
            stage[s] = returned[j, s]
        spot = lax.broadcasted_iota(jnp.int32, (chunk_width, block), 0) + j * chunk_width
        for b in range(slots):
            at = slice(b * block, (b + 1) * block)
            here = (spot == rank[b]).astype(F32).astype(BF16)
            term = jnp.dot(
                stage[inverse[b]], here, preferred_element_type=F32
            ).astype(BF16)

            @pl.when(j == 0)
            def _():
                out[:, at] = term

            @pl.when(j > 0)
            def _():
                out[:, at] = out[:, at] + term

        return carry

    lax.fori_loop(0, chunks, expand, 0)

    @pl.when(has_before)
    def _():
        to_before(head, after, 0).wait_send()
        to_before(east_head, east_after, 2).wait_send()

    @pl.when(has_after)
    def _():
        to_after(tail, before, 1).wait_send()
        to_after(east_tail, east_before, 3).wait_send()

    for j in range(chunks):
        for delta in range(1, slots):
            inward(j, delta).wait_send()
            if not relay:
                homeward(j, delta).wait_send()
        if relay:
            to_mate(j).wait_send()
            to_hub(j).wait_send()
    if relay:

        @pl.when(inner_device)
        def _():
            for j in range(chunks):
                for k in range(2):
                    onward(j, k).wait_send()


def whole(count, memory=pltpu.VMEM):
    return [pl.BlockSpec(memory_space=memory)] * count


def body(spectrum, land_sea, owners, proj_weight, back_weight, ocean_vel, mixing, active_layers):
    comps, rows, width = spectrum.shape
    slots = lax.axis_size("spec")
    points = rows * width
    block = points // slots
    cap = block * 3 // 4
    chunk_width = 256 if cap % 256 == 0 else cap
    chunks = cap // chunk_width
    layers = mixing.shape[0]
    rank_rows = proj_weight.shape[0]
    padded = -(-comps // ROWS) * ROWS
    edge = 2 * width
    me = lax.axis_index("spec")

    table = np.zeros((slots, padded, 12), np.float32)
    table[:, :comps] = tap_table().reshape(slots, comps, 12)
    taps = lax.dynamic_index_in_dim(jnp.asarray(table), me, 0, False)
    drift_rows, stress_rows = coupling_tables(layers)
    zeros = np.zeros((6, K), np.float32)
    outer = constant_pieces(np.concatenate([drift_rows, zeros, zeros[:2]], 0))
    outer = jnp.asarray(
        np.ascontiguousarray(outer.reshape(outer.shape[0], slots, comps).transpose(1, 0, 2))
    )
    through = jnp.dot(
        jnp.asarray(np.concatenate([source_step * drift_rows, stress_rows, zeros], 0)),
        back_weight.astype(F32),
        precision=lax.Precision.HIGHEST,
    )
    inner = pieces(through)
    proj = jnp.transpose(proj_weight.reshape(rank_rows, slots, comps), (1, 0, 2))
    back = back_weight.reshape(slots, comps, rank_rows)

    land = land_sea.astype(F32).reshape(slots, 1, block)
    covers = (owners[None, :] == jnp.arange(slots, dtype=jnp.int32)[:, None]).astype(jnp.int32)
    inverse = jnp.sum(covers * jnp.arange(slots, dtype=jnp.int32)[None], 1)
    place = jnp.broadcast_to(covers.astype(F32)[:, :, None, None], (slots, slots, 1, block))
    sea = land_sea.reshape(slots, block)
    rank = jnp.where(sea > 0, jnp.cumsum(sea, 1) - 1, -1).reshape(slots, 1, block)
    my_rank = lax.dynamic_index_in_dim(rank, owners[me], 0, False)

    velocity = ocean_vel.reshape(2, layers, block)
    mixing_local = mixing.reshape(layers, block)
    active = active_layers.reshape(1, block)
    state = spectrum.reshape(comps, points)
    pay_rows = inner.shape[0] // 3
    exchange = pltpu.VMEM((chunks, slots, comps, chunk_width), BF16)
    relay = []
    for _ in range(STEPS):
        state, velocity = pl.pallas_call(
            functools.partial(step_kernel, width),
            out_shape=(
                jax.ShapeDtypeStruct((comps, points), BF16),
                jax.ShapeDtypeStruct((2, layers, block), F32),
            ),
            in_specs=whole(2, pltpu.SMEM) + whole(13),
            out_specs=tuple(whole(2)),
            scratch_shapes=[
                pltpu.VMEM((slots, padded, block + 2 * edge), BF16),
                pltpu.VMEM((slots, 1, block + 2 * edge), F32),
                pltpu.VMEM((slots, 1, block), F32),
                pltpu.VMEM((padded, block), BF16),
                pltpu.VMEM((slots, chunks, comps, chunk_width), BF16),
                exchange,
                exchange,
                exchange,
                pltpu.VMEM((slots, comps, chunk_width), BF16),
                pltpu.VMEM((chunks, pay_rows, chunk_width), F32),
                pltpu.VMEM((2, block), F32),
                pltpu.VMEM((slots, 2, block), F32),
            ]
            + [pltpu.VMEM((comps, edge), BF16)] * 4
            + [pltpu.VMEM((1, edge), F32)] * 4
            + [pltpu.SemaphoreType.DMA((chunks, slots))] * 4
            + [pltpu.SemaphoreType.DMA((slots,))] * 2
            + [pltpu.SemaphoreType.DMA((4,))] * 2
            + relay,
            compiler_params=pltpu.CompilerParams(
                vmem_limit_bytes=VMEM_LIMIT, collective_id=0, has_side_effects=True
            ),
            name="step",
        )(owners, inverse, state, land, place, rank, my_rank, taps, proj, outer, back, inner,
          velocity, mixing_local, active)
    return (state.reshape(comps, rows, width), velocity.reshape(ocean_vel.shape))


def solution(mesh):
    placed = (
        P("spec", "space", None),
        P("space", None),
        P(),
        P(),
        P(),
        P(None, None, "spec", "space", None),
        P(None, "spec", "space", None),
        P("spec", "space", None),
    )
    return jax.shard_map(
        body,
        mesh=mesh,
        in_specs=placed,
        out_specs=(P("spec", "space", None), P(None, None, "spec", "space", None)),
        check_vma=False,
    )
```
